256 devices in a mesh: row: 8 (over x, core), col: 32 (over z, y).
Axes of the slice: x: 4, y: 4, z: 8, core: 2. Of those that a mesh axis runs over, the one named last changes fastest.
Arguments:
- inputs: bfloat16 [1024, 8192], P('col', 'row'), may hold values from -6 to 6
- target: bfloat16 [1024, 8192], P(None, 'row'), may hold values from -6 to 6
- gate_weight: bfloat16 [8192, 16384], P('row', 'col'), may hold values from -0.0625 to 0.0625
- up_weight: bfloat16 [8192, 16384], P('row', 'col'), may hold values from -0.0625 to 0.0625
- down_weight: bfloat16 [16384, 8192], P('col', 'row'), may hold values from -0.046875 to 0.046875
Outputs:
- output: bfloat16 [1024, 8192], P('col', 'row')
- grad_inputs: bfloat16 [1024, 8192], P('col', 'row')
- grad_gate_weight: bfloat16 [8192, 16384], P('row', 'col')
- grad_up_weight: bfloat16 [8192, 16384], P('row', 'col')
- grad_down_weight: bfloat16 [16384, 8192], P('col', 'row')
The draws below stay inside these ranges and needn't reach their ends.
All inputs are finite; a program needn't handle non-finite values.
Results may differ from the reference program's by a relative error of at most 0.0065.
Values may be sent and summed in bfloat16 or wider, within the bound.
No kernel may reach another device: no remote copies, remote signals or barrier semaphores. Data moves between devices by JAX's collectives and lax.ppermute only.
A program may use at most 64 MiB of HBM per device.

```python
import jax
import jax.numpy as jnp

D = 8192
FF = 16384
TOKENS = 1024


def block_levels(own_key, dims, split, least, high):
    factor_of = 1.0
    for axis_at, shards_of in split:
        draws = jax.random.uniform(jax.random.fold_in(jax.random.fold_in(own_key, 6), axis_at), (shards_of,), jnp.float32, least / len(split), high / len(split))
        factor_of = factor_of * jnp.repeat(jnp.exp(draws), dims[axis_at] // shards_of).reshape((-1,) + (1,) * (len(dims) - 1 - axis_at))
    return factor_of


def normal_values(stream_key, extent, scale, most, cuts=(), kind=jnp.bfloat16):
    values = jax.random.normal(stream_key, extent, jnp.float32) * scale
    if len(cuts) > 0:
        values = block_levels(stream_key, extent, cuts, -0.22, 0.18) * values
    return jnp.clip(values, min=-most, max=most).astype(kind)


def setup_inputs(seed: int = 0) -> dict:
    key_of = jax.random.split(jax.random.key(seed), 6)
    return {
        "inputs": normal_values(key_of[0], (TOKENS, D), 1.0, 6.0, ((0, 32), (1, 8))),
        "target": normal_values(key_of[1], (TOKENS, D), 1.0, 6.0, ((1, 8),)),
        "gate_weight": normal_values(key_of[2], (D, FF), D ** -0.5, 0.0625, ((0, 8), (1, 32))),
        "up_weight": normal_values(key_of[3], (D, FF), D ** -0.5, 0.0625, ((0, 8), (1, 32))),
        "down_weight": normal_values(key_of[4], (FF, D), FF ** -0.5, 0.046875, ((0, 32), (1, 8))),
    }


def reference(inputs, target, gate_weight, up_weight, down_weight):
    gate_act = jnp.dot(inputs, gate_weight, preferred_element_type=jnp.float32)
    up_act = jnp.dot(inputs, up_weight, preferred_element_type=jnp.float32)
    sigma = jax.nn.sigmoid(gate_act)
    silu_val = gate_act * sigma
    hidden = (silu_val * up_act).astype(jnp.bfloat16)
    result = jnp.dot(hidden, down_weight, preferred_element_type=jnp.float32)
    output = result.astype(jnp.bfloat16)
    error = (result - target.astype(jnp.float32)).astype(jnp.bfloat16)
    grad_down_weight = jnp.dot(hidden.T, error, preferred_element_type=jnp.float32).astype(jnp.bfloat16)
    grad_hidden = jnp.dot(error, down_weight.T, preferred_element_type=jnp.float32)
    grad_gate = (grad_hidden * up_act * sigma * (1.0 + gate_act * (1.0 - sigma))).astype(jnp.bfloat16)
    grad_up = (grad_hidden * silu_val).astype(jnp.bfloat16)
    grad_gate_weight = jnp.dot(inputs.T, grad_gate, preferred_element_type=jnp.float32).astype(jnp.bfloat16)
    grad_up_weight = jnp.dot(inputs.T, grad_up, preferred_element_type=jnp.float32).astype(jnp.bfloat16)
    grad_inputs = (jnp.dot(grad_gate, gate_weight.T, preferred_element_type=jnp.float32)
                   + jnp.dot(grad_up, up_weight.T, preferred_element_type=jnp.float32)).astype(jnp.bfloat16)
    return output, grad_inputs, grad_gate_weight, grad_up_weight, grad_down_weight
```

```python
import jax
import jax.numpy as jnp
from jax import lax
from jax.sharding import Mesh, PartitionSpec as P

F32 = jnp.float32
BF16 = jnp.bfloat16
NX, NC, NZ, NY = 4, 2, 8, 4


def contract_first(left, right):
    return lax.dot_general(left, right, (((0,), (0,)), ((), ())), preferred_element_type=F32)


def contract_last(left, right):
    return lax.dot_general(left, right, (((1,), (1,)), ((), ())), preferred_element_type=F32)


def exchange(val, axis):
    return lax.all_to_all(val, axis, split_axis=0, concat_axis=0, tiled=True)


def scatter_sum(part, axis, size):
    rows, cols = part.shape
    got = exchange(part.astype(BF16), axis).reshape(size, rows // size, cols)
    return jnp.sum(got.astype(F32), axis=0)


def spread(own, axis, size):
    rows, cols = own.shape
    return exchange(jnp.broadcast_to(own[None], (size, rows, cols)).reshape(size * rows, cols), axis)


def gather_col(own):
    return lax.all_gather(spread(own, "z", NZ), "y", axis=0, tiled=True)


def scatter_col(part):
    return scatter_sum(scatter_sum(part, "y", NY), "z", NZ)


def swap_core(val):
    return lax.ppermute(val, "core", [(0, 1), (1, 0)])


def scatter_row(part):
    half = part.shape[0] // NC
    core = lax.axis_index("core")
    mine = lax.dynamic_slice_in_dim(part, core * half, half, 0)
    other = lax.dynamic_slice_in_dim(part, (1 - core) * half, half, 0)
    both = mine + swap_core(other.astype(BF16)).astype(F32)
    return scatter_sum(both, "x", NX)


def gather_row(own):
    mine = spread(own, "x", NX)
    other = swap_core(mine)
    first = lax.axis_index("core") == 0
    return jnp.concatenate([jnp.where(first, mine, other), jnp.where(first, other, mine)], axis=0)


def gate_grads(hidden_grad, gate_act, up_act):
    sigma = jax.nn.sigmoid(gate_act)
    silu_val = gate_act * sigma
    grad_gate = hidden_grad * up_act * sigma * (1.0 + gate_act * (1.0 - sigma))
    grad_up = hidden_grad * silu_val
    return jnp.concatenate([grad_gate.astype(BF16), grad_up.astype(BF16)], axis=1)


def body(inputs, target, gate_weight, up_weight, down_weight):
    wide = gate_weight.shape[1]
    tok_own = inputs.shape[0]
    tokens_all = gather_col(inputs)
    gate_part = jnp.dot(tokens_all, gate_weight, preferred_element_type=F32)
    up_part = jnp.dot(tokens_all, up_weight, preferred_element_type=F32)
    acts = scatter_row(jnp.concatenate([gate_part, up_part], axis=1))
    gate_own, up_own = acts[:, :wide], acts[:, wide:]
    hidden_own = (jax.nn.silu(gate_own) * up_own).astype(BF16)
    hidden_all = gather_row(hidden_own)
    result_part = jnp.dot(hidden_all, down_weight, preferred_element_type=F32)
    result_own = scatter_col(result_part)
    offset = (lax.axis_index("z") * NY + lax.axis_index("y")) * tok_own
    target_own = lax.dynamic_slice_in_dim(target, offset, tok_own, 0)
    error_own = (result_own - target_own.astype(F32)).astype(BF16)
    output = result_own.astype(BF16)
    error_all = gather_col(error_own)
    hidden_grad = scatter_row(contract_last(error_all, down_weight))
    grads_all = gather_row(gate_grads(hidden_grad, gate_own, up_own))
    gate_grad_all, up_grad_all = grads_all[:, :wide], grads_all[:, wide:]
    input_grad_part = contract_last(gate_grad_all, gate_weight) + contract_last(
        up_grad_all, up_weight
    )
    grad_inputs = scatter_col(input_grad_part).astype(BF16)
    grad_down_weight = contract_first(hidden_all, error_all).astype(BF16)
    grad_gate_weight = contract_first(tokens_all, gate_grad_all).astype(BF16)
    grad_up_weight = contract_first(tokens_all, up_grad_all).astype(BF16)
    return (output, grad_inputs, grad_gate_weight, grad_up_weight, grad_down_weight)


def solution(mesh):
    fine = Mesh(mesh.devices.reshape(NX, NC, NZ, NY), ("x", "core", "z", "y"))
    row, col = ("x", "core"), ("z", "y")
    placed = (P(col, row), P(None, row), P(row, col), P(row, col), P(col, row))
    return jax.shard_map(
        body,
        mesh=fine,
        in_specs=placed,
        out_specs=(P(col, row), P(col, row), P(row, col), P(row, col), P(col, row)),
        check_vma=False,
    )
```

```python
import jax
import jax.numpy as jnp
from jax import lax
from jax.sharding import Mesh, PartitionSpec as P

F32 = jnp.float32
BF16 = jnp.bfloat16
NX, NC, NZ, NY = 4, 2, 8, 4


def contract_first(left, right):
    return lax.dot_general(left, right, (((0,), (0,)), ((), ())), preferred_element_type=F32)


def contract_last(left, right):
    return lax.dot_general(left, right, (((1,), (1,)), ((), ())), preferred_element_type=F32)


def matmul(left, right):
    return jnp.dot(left, right, preferred_element_type=F32)


def shift(val, axis, size, by):
    return lax.ppermute(val, axis, [(at, (at + by) % size) for at in range(size)])


def exchange(val, axis):
    return lax.all_to_all(val, axis, split_axis=0, concat_axis=0, tiled=True)


def rows_at(val, block, size):
    return lax.dynamic_slice_in_dim(val, block * size, size, 0)


def gather_z(own):
    rows, cols = own.shape
    return exchange(jnp.broadcast_to(own[None], (NZ, rows, cols)).reshape(NZ * rows, cols), "z")


def scatter_z(part):
    rows, cols = part.shape
    got = exchange(part.astype(BF16), "z").reshape(NZ, rows // NZ, cols)
    return jnp.sum(got.astype(F32), axis=0)


def gather_y(own):
    half = own.shape[0] // 2
    low = shift(own, "y", NY, 1)
    high = shift(own, "y", NY, -1)
    far = (shift(low[:half], "y", NY, 1), shift(high[half:], "y", NY, -1))
    return jnp.concatenate([own, low, high], axis=0), jnp.concatenate(far, axis=0)


def scatter_y(near, far):
    rows = far.shape[0]
    total = near[:rows]
    total = total + shift(near[rows : 2 * rows].astype(BF16), "y", NY, -1).astype(F32)
    total = total + shift(near[2 * rows :].astype(BF16), "y", NY, 1).astype(F32)
    return total + shift(far.astype(BF16), "y", NY, 2).astype(F32)


def scatter_row(part):
    half = part.shape[0] // NC
    block = half // NX
    core, at = lax.axis_index("core"), lax.axis_index("x")
    other = shift(rows_at(part, 1 - core, half).astype(BF16), "core", NC, 1)
    both = rows_at(part, core, half) + other.astype(F32)
    sent = [
        shift(rows_at(both, (at + by) % NX, block).astype(BF16), "x", NX, by) for by in (1, 3, 2)
    ]
    total = rows_at(both, at, block)
    for val in sent:
        total = total + val.astype(F32)
    return total


def gather_row(own):
    at = lax.axis_index("x")
    got = [own] + [shift(own, "x", NX, -by) for by in (1, 2, 3)]
    ring = jnp.concatenate(got + got, axis=0)
    rows = own.shape[0]
    mine = lax.dynamic_slice_in_dim(ring, ((NX - at) % NX) * rows, NX * rows, 0)
    other = shift(mine, "core", NC, 1)
    first = lax.axis_index("core") == 0
    return jnp.concatenate([jnp.where(first, mine, other), jnp.where(first, other, mine)], axis=0)


def gate_grads(hidden_grad, gate_act, up_act):
    sigma = jax.nn.sigmoid(gate_act)
    silu_val = gate_act * sigma
    grad_gate = hidden_grad * up_act * sigma * (1.0 + gate_act * (1.0 - sigma))
    grad_up = hidden_grad * silu_val
    return jnp.concatenate([grad_gate.astype(BF16), grad_up.astype(BF16)], axis=1)


def body(inputs, target, gate_weight, up_weight, down_weight):
    wide = gate_weight.shape[1]
    tok_own = inputs.shape[0]
    tokens = gather_y(gather_z(inputs))
    acts, hidden, result = [], [], []
    for part in tokens:
        act = scatter_row(
            jnp.concatenate([matmul(part, gate_weight), matmul(part, up_weight)], axis=1)
        )
        acts.append(act)
        hid = gather_row((jax.nn.silu(act[:, :wide]) * act[:, wide:]).astype(BF16))
        hidden.append(hid)
        result.append(matmul(hid, down_weight))
    result_own = scatter_z(scatter_y(*result))
    offset = (lax.axis_index("z") * NY + lax.axis_index("y")) * tok_own
    target_own = lax.dynamic_slice_in_dim(target, offset, tok_own, 0)
    error_own = (result_own - target_own.astype(F32)).astype(BF16)
    output = result_own.astype(BF16)
    errors = gather_y(gather_z(error_own))
    gate_grad, up_grad, input_grad = [], [], []
    for part, act in zip(errors, acts):
        hidden_grad = scatter_row(contract_last(part, down_weight))
        grads = gather_row(gate_grads(hidden_grad, act[:, :wide], act[:, wide:]))
        gate_grad.append(grads[:, :wide])
        up_grad.append(grads[:, wide:])
        input_grad.append(
            contract_last(grads[:, :wide], gate_weight) + contract_last(grads[:, wide:], up_weight)
        )
    grad_inputs = scatter_z(scatter_y(*input_grad)).astype(BF16)

    def summed(left, right):
        return sum(contract_first(a, b) for a, b in zip(left, right)).astype(BF16)

    return (
        output,
        grad_inputs,
        summed(tokens, gate_grad),
        summed(tokens, up_grad),
        summed(hidden, errors),
    )


def solution(mesh):
    fine = Mesh(mesh.devices.reshape(NX, NC, NZ, NY), ("x", "core", "z", "y"))
    row, col = ("x", "core"), ("z", "y")
    placed = (P(col, row), P(None, row), P(row, col), P(row, col), P(col, row))
    return jax.shard_map(
        body,
        mesh=fine,
        in_specs=placed,
        out_specs=(P(col, row), P(col, row), P(row, col), P(row, col), P(col, row)),
        check_vma=False,
    )
```

```python
import jax
import jax.numpy as jnp
from jax import lax
from jax.sharding import Mesh, PartitionSpec as P

F32 = jnp.float32
BF16 = jnp.bfloat16
NX, NC, NZ, NY = 4, 2, 8, 4
AXES = ("x", "core", "z", "y")
CHUNKS = ((0, 1, 2, 3),)


def place(x, core, z, y):
    return ((x * NC + core) * NZ + z) * NY + y


Z_GROUPS = [
    [place(x, core, at ^ (core * NX + x), y) for at in range(NZ)]
    for x in range(NX)
    for core in range(NC)
    for y in range(NY)
]


def contract_first(left, right):
    return lax.dot_general(left, right, (((0,), (0,)), ((), ())), preferred_element_type=F32)


def contract_last(left, right):
    return lax.dot_general(left, right, (((1,), (1,)), ((), ())), preferred_element_type=F32)


def matmul(left, right):
    return jnp.dot(left, right, preferred_element_type=F32)


def shift_y(val, by):
    return lax.ppermute(val, "y", [(at, (at + by) % NY) for at in range(NY)])


def swap_x(val, flip):
    return lax.ppermute(val, "x", [(at, at ^ flip) for at in range(NX)])


def swap_core(val):
    return lax.ppermute(val, "core", [(0, 1), (1, 0)])


def exchange_z(val):
    return lax.all_to_all(
        val, AXES, split_axis=0, concat_axis=0, axis_index_groups=Z_GROUPS, tiled=True
    )


def gather_z(own):
    rows, cols = own.shape
    return exchange_z(jnp.broadcast_to(own[None], (NZ, rows, cols)).reshape(NZ * rows, cols))


def scatter_z(part):
    rows, cols = part.shape
    got = exchange_z(part.astype(BF16)).reshape(NZ, rows // NZ, cols)
    return jnp.sum(got.astype(F32), axis=0)


def gather_y(own):
    half = own.shape[0] // 2
    low = shift_y(own, 1)
    high = shift_y(own, -1)
    far = jnp.concatenate([shift_y(low[:half], 1), shift_y(high[half:], -1)], axis=0)
    return [own, low, high, far]


def scatter_y(blocks):
    own, low, high, far = blocks
    total = own
    total = total + shift_y(low.astype(BF16), -1).astype(F32)
    total = total + shift_y(high.astype(BF16), 1).astype(F32)
    return total + shift_y(far.astype(BF16), 2).astype(F32)


def after(val, dep):
    return lax.optimization_barrier((val, dep))[0]


def cut(val, tok):
    return val.reshape(-1, NZ, tok, val.shape[1])


def core_step(parts):
    send = jnp.stack([part[:, NX:].astype(BF16) for part in parts])
    return jnp.stack([part[:, :NX] for part in parts]) + swap_core(send).astype(F32)


def x_send(both):
    return [swap_x(both[:, :, flip].astype(BF16), flip) for flip in range(1, NX)]


def x_sum(both, got):
    total = both[:, :, 0]
    for val in got:
        total = total + val.astype(F32)
    return total


def x_spread(own):
    return jnp.stack([own] + [swap_x(own, flip) for flip in range(1, NX)], axis=2)


def core_spread(mine):
    full = jnp.concatenate([mine, swap_core(mine)], axis=2)
    return [val.reshape(-1, val.shape[-1]) for val in full]


def row_phase(chunks, tok, first, middle, last):
    order = range(len(chunks))
    both, own, full, out = [], [], [], []
    for k in order:
        tokens = chunks[k] if k == 0 else after(chunks[k], both[k - 1])
        both.append(core_step([cut(part, tok) for part in first(tokens)]))
    sums = []
    for k in order:
        sums.append(x_sum(both[k], x_send(both[k])))
        own.append(middle(k, sums[k]))
    for k in order:
        full.append(core_spread(x_spread(own[k])))
    for k in order:
        out.append(last(full[k]))
    return sums, full, out


def join(blocks):
    return [
        jnp.concatenate([blocks[at] for at in chunk], axis=0) if len(chunk) > 1 else blocks[chunk[0]]
        for chunk in CHUNKS
    ]


def split(parts):
    blocks = {}
    for chunk, part in zip(CHUNKS, parts):
        rows = part.shape[0] // len(chunk)
        for at, which in enumerate(chunk):
            blocks[which] = part[at * rows : (at + 1) * rows]
    return [blocks[at] for at in range(NY)]


def gate_grads(hidden_grad, gate_act, up_act):
    sigma = jax.nn.sigmoid(gate_act)
    silu_val = gate_act * sigma
    grad_gate = hidden_grad * up_act * sigma * (1.0 + gate_act * (1.0 - sigma))
    grad_up = hidden_grad * silu_val
    return jnp.stack([grad_gate.astype(BF16), grad_up.astype(BF16)])


def body(inputs, target, gate_weight, up_weight, down_weight):
    tok_own = inputs.shape[0]
    tokens = join(gather_y(gather_z(inputs)))
    acts, hidden, result = row_phase(
        tokens,
        tok_own,
        lambda val: (matmul(val, gate_weight), matmul(val, up_weight)),
        lambda k, act: (jax.nn.silu(act[0]) * act[1]).astype(BF16)[None],
        lambda full: matmul(full[0], down_weight),
    )
    result_own = scatter_z(scatter_y(split(result)))
    offset = (lax.axis_index("z") * NY + lax.axis_index("y")) * tok_own
    target_own = lax.dynamic_slice_in_dim(target, offset, tok_own, 0)
    error_own = (result_own - target_own.astype(F32)).astype(BF16)
    output = result_own.astype(BF16)
    errors = join(gather_y(gather_z(error_own)))
    _, grads, input_grad = row_phase(
        errors,
        tok_own,
        lambda val: (contract_last(val, down_weight),),
        lambda k, grad: gate_grads(grad[0], acts[k][0], acts[k][1]),
        lambda full: contract_last(full[0], gate_weight) + contract_last(full[1], up_weight),
    )
    grad_inputs = scatter_z(scatter_y(split(input_grad))).astype(BF16)

    def summed(left, right):
        return sum(contract_first(a, b) for a, b in zip(left, right)).astype(BF16)

    return (
        output,
        grad_inputs,
        summed(tokens, [val[0] for val in grads]),
        summed(tokens, [val[1] for val in grads]),
        summed([val[0] for val in hidden], errors),
    )


def solution(mesh):
    fine = Mesh(mesh.devices.reshape(NX, NC, NZ, NY), AXES)
    row, col = ("x", "core"), ("z", "y")
    placed = (P(col, row), P(None, row), P(row, col), P(row, col), P(col, row))
    return jax.shard_map(
        body,
        mesh=fine,
        in_specs=placed,
        out_specs=(P(col, row), P(col, row), P(row, col), P(row, col), P(col, row)),
        check_vma=False,
    )
```

```python
import jax
import jax.numpy as jnp
from jax import lax
from jax.sharding import Mesh, PartitionSpec as P

F32 = jnp.float32
BF16 = jnp.bfloat16
NX, NC, NZ, NY = 4, 2, 8, 4
AXES = ("x", "core", "z", "y")
CHUNKS = ((0, 1, 2, 3),)


def place(x, core, z, y):
    return ((x * NC + core) * NZ + z) * NY + y


Z_GROUPS = [
    [place(x, core, at ^ (core * NX + x), y) for at in range(NZ)]
    for x in range(NX)
    for core in range(NC)
    for y in range(NY)
]


def contract_first(left, right):
    return lax.dot_general(left, right, (((0,), (0,)), ((), ())), preferred_element_type=F32)


def contract_last(left, right):
    return lax.dot_general(left, right, (((1,), (1,)), ((), ())), preferred_element_type=F32)


def matmul(left, right):
    return jnp.dot(left, right, preferred_element_type=F32)


def shift_y(val, by):
    return lax.ppermute(val, "y", [(at, (at + by) % NY) for at in range(NY)])


def swap_x(val, flip):
    return lax.ppermute(val, "x", [(at, at ^ flip) for at in range(NX)])


def swap_core(val):
    return lax.ppermute(val, "core", [(0, 1), (1, 0)])


def exchange_z(val):
    return lax.all_to_all(
        val, AXES, split_axis=0, concat_axis=0, axis_index_groups=Z_GROUPS, tiled=True
    )


def gather_z(own):
    rows, cols = own.shape
    return exchange_z(jnp.broadcast_to(own[None], (NZ, rows, cols)).reshape(NZ * rows, cols))


def scatter_z(part):
    rows, cols = part.shape
    got = exchange_z(part.astype(BF16)).reshape(NZ, rows // NZ, cols)
    return jnp.sum(got.astype(F32), axis=0)


def gather_y(own):
    half = own.shape[0] // 2
    upper, lower = own[:half], own[half:]
    low_a = shift_y(upper, 1)
    high_b = shift_y(lower, -1)
    low_b = shift_y(lower, 1)
    high_a = shift_y(upper, -1)
    far_a = shift_y(low_a, 1)
    far_b = shift_y(high_b, -1)
    return [own, *(jnp.concatenate(val, axis=0) for val in ((low_a, low_b), (high_a, high_b), (far_a, far_b)))]


def scatter_y(blocks):
    own, low, high, far = (val.astype(BF16) for val in blocks)
    half = own.shape[0] // 2
    upper = shift_y(far[:half], 1).astype(F32)
    lower = shift_y(far[half:], -1).astype(F32)
    high_b = shift_y(high[half:], 1).astype(F32)
    low_a = shift_y(low[:half], -1).astype(F32)
    high_a = shift_y((blocks[2][:half] + upper).astype(BF16), 1).astype(F32)
    low_b = shift_y((blocks[1][half:] + lower).astype(BF16), -1).astype(F32)
    return jnp.concatenate([blocks[0][:half] + low_a + high_a, blocks[0][half:] + high_b + low_b], axis=0)


def after(val, dep):
    return lax.optimization_barrier((val, dep))[0]


def cut(val, tok):
    return val.reshape(-1, NZ, tok, val.shape[1])


def core_step(parts):
    send = jnp.stack([part[:, NX:].astype(BF16) for part in parts])
    return jnp.stack([part[:, :NX] for part in parts]) + swap_core(send).astype(F32)


def x_send(both):
    return [swap_x(both[:, :, flip].astype(BF16), flip) for flip in range(1, NX)]


def x_sum(both, got):
    total = both[:, :, 0]
    for val in got:
        total = total + val.astype(F32)
    return total


def x_spread(own):
    return jnp.stack([own] + [swap_x(own, flip) for flip in range(1, NX)], axis=2)


def core_spread(mine):
    full = jnp.concatenate([mine, swap_core(mine)], axis=2)
    return [val.reshape(-1, val.shape[-1]) for val in full]


def row_phase(chunks, tok, first, middle, last):
    order = range(len(chunks))
    both, own, full, out = [], [], [], []
    for k in order:
        tokens = chunks[k] if k == 0 else after(chunks[k], both[k - 1])
        both.append(core_step([cut(part, tok) for part in first(tokens)]))
    sums = []
    for k in order:
        sums.append(x_sum(both[k], x_send(both[k])))
        own.append(middle(k, sums[k]))
    for k in order:
        full.append(core_spread(x_spread(own[k])))
    for k in order:
        out.append(last(full[k]))
    return sums, full, out


def join(blocks):
    return [
        jnp.concatenate([blocks[at] for at in chunk], axis=0) if len(chunk) > 1 else blocks[chunk[0]]
        for chunk in CHUNKS
    ]


def split(parts):
    blocks = {}
    for chunk, part in zip(CHUNKS, parts):
        rows = part.shape[0] // len(chunk)
        for at, which in enumerate(chunk):
            blocks[which] = part[at * rows : (at + 1) * rows]
    return [blocks[at] for at in range(NY)]


def gate_grads(hidden_grad, gate_act, up_act):
    sigma = jax.nn.sigmoid(gate_act)
    silu_val = gate_act * sigma
    grad_gate = hidden_grad * up_act * sigma * (1.0 + gate_act * (1.0 - sigma))
    grad_up = hidden_grad * silu_val
    return jnp.stack([grad_gate.astype(BF16), grad_up.astype(BF16)])


def body(inputs, target, gate_weight, up_weight, down_weight):
    tok_own = inputs.shape[0]
    tokens = join(gather_y(gather_z(inputs)))
    acts, hidden, result = row_phase(
        tokens,
        tok_own,
        lambda val: (matmul(val, gate_weight), matmul(val, up_weight)),
        lambda k, act: (jax.nn.silu(act[0]) * act[1]).astype(BF16)[None],
        lambda full: matmul(full[0], down_weight),
    )
    result_own = scatter_z(scatter_y(split(result)))
    offset = (lax.axis_index("z") * NY + lax.axis_index("y")) * tok_own
    target_own = lax.dynamic_slice_in_dim(target, offset, tok_own, 0)
    error_own = (result_own - target_own.astype(F32)).astype(BF16)
    output = result_own.astype(BF16)
    errors = join(gather_y(gather_z(error_own)))
    _, grads, input_grad = row_phase(
        errors,
        tok_own,
        lambda val: (contract_last(val, down_weight),),
        lambda k, grad: gate_grads(grad[0], acts[k][0], acts[k][1]),
        lambda full: contract_last(full[0], gate_weight) + contract_last(full[1], up_weight),
    )
    grad_inputs = scatter_z(scatter_y(split(input_grad))).astype(BF16)

    def summed(left, right):
        return sum(contract_first(a, b) for a, b in zip(left, right)).astype(BF16)

    return (
        output,
        grad_inputs,
        summed(tokens, [val[0] for val in grads]),
        summed(tokens, [val[1] for val in grads]),
        summed([val[0] for val in hidden], errors),
    )


def solution(mesh):
    fine = Mesh(mesh.devices.reshape(NX, NC, NZ, NY), AXES)
    row, col = ("x", "core"), ("z", "y")
    placed = (P(col, row), P(None, row), P(row, col), P(row, col), P(col, row))
    return jax.shard_map(
        body,
        mesh=fine,
        in_specs=placed,
        out_specs=(P(col, row), P(col, row), P(row, col), P(row, col), P(col, row)),
        check_vma=False,
    )
```

```python
import jax
import jax.numpy as jnp
from jax import lax
from jax.sharding import Mesh, PartitionSpec as P

F32 = jnp.float32
BF16 = jnp.bfloat16
NX, NC, NZ, NY = 4, 2, 8, 4
AXES = ("x", "core", "z", "y")
CHUNKS = ((0, 1, 2, 3),)


def place(x, core, z, y):
    return ((x * NC + core) * NZ + z) * NY + y


Z_GROUPS = [
    [place(x, core, at ^ (core * NX + x), y) for at in range(NZ)]
    for x in range(NX)
    for core in range(NC)
    for y in range(NY)
]


def contract_first(left, right):
    return lax.dot_general(left, right, (((0,), (0,)), ((), ())), preferred_element_type=F32)


def contract_last(left, right):
    return lax.dot_general(left, right, (((1,), (1,)), ((), ())), preferred_element_type=F32)


def matmul(left, right):
    return jnp.dot(left, right, preferred_element_type=F32)


def shift_y(val, by):
    return lax.ppermute(val, "y", [(at, (at + by) % NY) for at in range(NY)])


def swap_x(val, flip):
    return lax.ppermute(val, "x", [(at, at ^ flip) for at in range(NX)])


def swap_core(val):
    return lax.ppermute(val, "core", [(0, 1), (1, 0)])


def exchange_z(val):
    return lax.all_to_all(
        val, AXES, split_axis=0, concat_axis=0, axis_index_groups=Z_GROUPS, tiled=True
    )


def gather_z(own):
    rows, cols = own.shape
    return exchange_z(jnp.broadcast_to(own[None], (NZ, rows, cols)).reshape(NZ * rows, cols))


def scatter_z(part):
    rows, cols = part.shape
    got = exchange_z(part.astype(BF16)).reshape(NZ, rows // NZ, cols)
    return jnp.sum(got.astype(F32), axis=0)


def gather_y(own):
    half = own.shape[0] // 2
    upper, lower = own[:half], own[half:]
    low_a = shift_y(upper, 1)
    high_b = shift_y(lower, -1)
    low_b = shift_y(lower, 1)
    high_a = shift_y(upper, -1)
    far_a = shift_y(low_a, 1)
    far_b = shift_y(high_b, -1)
    return [own, *(jnp.concatenate(val, axis=0) for val in ((low_a, low_b), (high_a, high_b), (far_a, far_b)))]


def scatter_y(blocks):
    own, low, high, far = blocks
    half = own.shape[0] // 2
    upper = shift_y(far[:half].astype(BF16), 1)
    lower = shift_y(far[half:].astype(BF16), -1)
    high_b = shift_y(high[half:].astype(BF16), 1)
    low_a = shift_y(low[:half].astype(BF16), -1)
    high_a = shift_y((high[:half] + upper.astype(F32)).astype(BF16), 1)
    low_b = shift_y((low[half:] + lower.astype(F32)).astype(BF16), -1)
    low = jnp.concatenate([low_a, low_b], axis=0)
    high = jnp.concatenate([high_a, high_b], axis=0)
    return own + low.astype(F32) + high.astype(F32)


def after(val, dep):
    return lax.optimization_barrier((val, dep))[0]


def cut(val, tok):
    return val.reshape(-1, NZ, tok, val.shape[1])


def core_step(parts):
    send = jnp.stack([part[:, NX:].astype(BF16) for part in parts])
    return jnp.stack([part[:, :NX] for part in parts]) + swap_core(send).astype(F32)


def x_send(both):
    return [swap_x(both[:, :, flip].astype(BF16), flip) for flip in range(1, NX)]


def x_sum(both, got):
    total = both[:, :, 0]
    for val in got:
        total = total + val.astype(F32)
    return total


def x_spread(own):
    return jnp.stack([own] + [swap_x(own, flip) for flip in range(1, NX)], axis=2)


def core_spread(mine):
    full = jnp.concatenate([mine, swap_core(mine)], axis=2)
    return [val.reshape(-1, val.shape[-1]) for val in full]


def row_phase(chunks, tok, first, middle, last):
    order = range(len(chunks))
    both, own, full, out = [], [], [], []
    for k in order:
        tokens = chunks[k] if k == 0 else after(chunks[k], both[k - 1])
        both.append(core_step([cut(part, tok) for part in first(tokens)]))
    sums = []
    for k in order:
        sums.append(x_sum(both[k], x_send(both[k])))
        own.append(middle(k, sums[k]))
    for k in order:
        full.append(core_spread(x_spread(own[k])))
    for k in order:
        out.append(last(full[k]))
    return sums, full, out


def join(blocks):
    return [
        jnp.concatenate([blocks[at] for at in chunk], axis=0) if len(chunk) > 1 else blocks[chunk[0]]
        for chunk in CHUNKS
    ]


def split(parts):
    blocks = {}
    for chunk, part in zip(CHUNKS, parts):
        rows = part.shape[0] // len(chunk)
        for at, which in enumerate(chunk):
            blocks[which] = part[at * rows : (at + 1) * rows]
    return [blocks[at] for at in range(NY)]


def gate_grads(hidden_grad, gate_act, up_act):
    sigma = jax.nn.sigmoid(gate_act)
    silu_val = gate_act * sigma
    grad_gate = hidden_grad * up_act * sigma * (1.0 + gate_act * (1.0 - sigma))
    grad_up = hidden_grad * silu_val
    return jnp.stack([grad_gate.astype(BF16), grad_up.astype(BF16)])


def body(inputs, target, gate_weight, up_weight, down_weight):
    tok_own = inputs.shape[0]
    tokens = join(gather_y(gather_z(inputs)))
    acts, hidden, result = row_phase(
        tokens,
        tok_own,
        lambda val: (matmul(val, gate_weight), matmul(val, up_weight)),
        lambda k, act: (jax.nn.silu(act[0]) * act[1]).astype(BF16)[None],
        lambda full: matmul(full[0], down_weight),
    )
    result_own = scatter_y(split(result))
    result_own = scatter_z(result_own)
    offset = (lax.axis_index("z") * NY + lax.axis_index("y")) * tok_own
    target_own = lax.dynamic_slice_in_dim(target, offset, tok_own, 0)
    error_own = (result_own - target_own.astype(F32)).astype(BF16)
    output = result_own.astype(BF16)
    errors = join(gather_y(gather_z(error_own)))
    _, grads, input_grad = row_phase(
        errors,
        tok_own,
        lambda val: (contract_last(val, down_weight),),
        lambda k, grad: gate_grads(grad[0], acts[k][0], acts[k][1]),
        lambda full: contract_last(full[0], gate_weight) + contract_last(full[1], up_weight),
    )
    grad_inputs = scatter_y(split(input_grad))
    grad_inputs = scatter_z(grad_inputs).astype(BF16)

    def summed(left, right):
        return sum(contract_first(a, b) for a, b in zip(left, right)).astype(BF16)

    return (
        output,
        grad_inputs,
        summed(tokens, [val[0] for val in grads]),
        summed(tokens, [val[1] for val in grads]),
        summed([val[0] for val in hidden], errors),
    )


def solution(mesh):
    fine = Mesh(mesh.devices.reshape(NX, NC, NZ, NY), AXES)
    row, col = ("x", "core"), ("z", "y")
    placed = (P(col, row), P(None, row), P(row, col), P(row, col), P(col, row))
    return jax.shard_map(
        body,
        mesh=fine,
        in_specs=placed,
        out_specs=(P(col, row), P(col, row), P(row, col), P(row, col), P(col, row)),
        check_vma=False,
    )
```

```python
import jax
import jax.numpy as jnp
from jax import lax
from jax.sharding import Mesh, PartitionSpec as P

F32 = jnp.float32
BF16 = jnp.bfloat16
NX, NC, NZ, NY = 4, 2, 8, 4
AXES = ("x", "core", "z", "y")
CHUNKS = ((0, 1, 2, 3),)


def place(x, core, z, y):
    return ((x * NC + core) * NZ + z) * NY + y


Z_GROUPS = [
    [place(x, core, at ^ (core * NX + x), y) for at in range(NZ)]
    for x in range(NX)
    for core in range(NC)
    for y in range(NY)
]


def contract_first(left, right):
    return lax.dot_general(left, right, (((0,), (0,)), ((), ())), preferred_element_type=F32)


def contract_last(left, right):
    return lax.dot_general(left, right, (((1,), (1,)), ((), ())), preferred_element_type=F32)


def matmul(left, right):
    return jnp.dot(left, right, preferred_element_type=F32)


def shift_y(val, by):
    return lax.ppermute(val, "y", [(at, (at + by) % NY) for at in range(NY)])


def swap_x(val, flip):
    return lax.ppermute(val, "x", [(at, at ^ flip) for at in range(NX)])


def swap_core(val):
    return lax.ppermute(val, "core", [(0, 1), (1, 0)])


def exchange_z(val):
    return lax.all_to_all(
        val, AXES, split_axis=0, concat_axis=0, axis_index_groups=Z_GROUPS, tiled=True
    )


def gather_z(own):
    rows, cols = own.shape
    return exchange_z(jnp.broadcast_to(own[None], (NZ, rows, cols)).reshape(NZ * rows, cols))


def scatter_z(part):
    rows, cols = part.shape
    got = exchange_z(part.astype(BF16)).reshape(NZ, rows // NZ, cols)
    return jnp.sum(got.astype(F32), axis=0)


def gather_y(own):
    half = own.shape[0] // 2
    upper, lower = own[:half], own[half:]
    low_a = shift_y(upper, 1)
    high_b = shift_y(lower, -1)
    low_b = shift_y(lower, 1)
    high_a = shift_y(upper, -1)
    far_a = shift_y(low_a, 1)
    far_b = shift_y(high_b, -1)
    pairs = ((low_a, low_b), (high_a, high_b), (far_a, far_b))
    return [own, *(jnp.concatenate(val, axis=0) for val in pairs)]


def scatter_y(blocks):
    own, low, high, far = blocks
    half = own.shape[0] // 2
    upper = shift_y(far[:half].astype(BF16), 1)
    lower = shift_y(far[half:].astype(BF16), -1)
    high_b = shift_y(high[half:].astype(BF16), 1)
    low_a = shift_y(low[:half].astype(BF16), -1)
    high_a = shift_y((high[:half] + upper.astype(F32)).astype(BF16), 1)
    low_b = shift_y((low[half:] + lower.astype(F32)).astype(BF16), -1)
    low = jnp.concatenate([low_a, low_b], axis=0)
    high = jnp.concatenate([high_a, high_b], axis=0)
    return own + low.astype(F32) + high.astype(F32)


def after(val, dep):
    return lax.optimization_barrier((val, dep))[0]


def cut(val, tok):
    return val.reshape(-1, NZ, tok, val.shape[1])


def core_step(parts):
    send = jnp.stack([part[:, NX:].astype(BF16) for part in parts])
    return jnp.stack([part[:, :NX] for part in parts]) + swap_core(send).astype(F32)


def x_send(both):
    one, two, three = (both[:, :, flip] for flip in range(1, NX))
    if both.shape[0] == 1:
        return [swap_x(val.astype(BF16), flip) for flip, val in ((1, one), (2, two), (3, three))]
    half = both.shape[1] // 2
    upper = swap_x(two[:, :half].astype(BF16), 1)
    lower = swap_x(two[:, half:].astype(BF16), 3)
    one_a = swap_x(one[:, :half].astype(BF16), 1)
    three_b = swap_x(three[:, half:].astype(BF16), 3)
    three_a = swap_x((three[:, :half] + upper.astype(F32)).astype(BF16), 3)
    one_b = swap_x((one[:, half:] + lower.astype(F32)).astype(BF16), 1)
    return [jnp.concatenate([one_a, one_b], axis=1), jnp.concatenate([three_a, three_b], axis=1)]


def x_sum(both, got):
    total = both[:, :, 0]
    for val in got:
        total = total + val.astype(F32)
    return total


def x_spread(own):
    if own.shape[0] == 1:
        return jnp.stack([own] + [swap_x(own, flip) for flip in range(1, NX)], axis=2)
    half = own.shape[1] // 2
    upper, lower = own[:, :half], own[:, half:]
    one_a = swap_x(upper, 1)
    three_b = swap_x(lower, 3)
    one_b = swap_x(lower, 1)
    three_a = swap_x(upper, 3)
    two_a = swap_x(one_a, 3)
    two_b = swap_x(three_b, 1)
    pairs = ((upper, lower), (one_a, one_b), (two_a, two_b), (three_a, three_b))
    return jnp.stack([jnp.concatenate(val, axis=1) for val in pairs], axis=2)


def core_spread(mine):
    full = jnp.concatenate([mine, swap_core(mine)], axis=2)
    return [val.reshape(-1, val.shape[-1]) for val in full]


def row_phase(chunks, tok, first, middle, last):
    order = range(len(chunks))
    both, own, full, out = [], [], [], []
    for k in order:
        tokens = chunks[k] if k == 0 else after(chunks[k], both[k - 1])
        both.append(core_step([cut(part, tok) for part in first(tokens)]))
    sums = []
    for k in order:
        sums.append(x_sum(both[k], x_send(both[k])))
        own.append(middle(k, sums[k]))
    for k in order:
        full.append(core_spread(x_spread(own[k])))
    for k in order:
        out.append(last(full[k]))
    return sums, full, out


def join(blocks):
    return [
        jnp.concatenate([blocks[at] for at in chunk], axis=0) if len(chunk) > 1 else blocks[chunk[0]]
        for chunk in CHUNKS
    ]


def split(parts):
    blocks = {}
    for chunk, part in zip(CHUNKS, parts):
        rows = part.shape[0] // len(chunk)
        for at, which in enumerate(chunk):
            blocks[which] = part[at * rows : (at + 1) * rows]
    return [blocks[at] for at in range(NY)]


def gate_grads(hidden_grad, gate_act, up_act):
    sigma = jax.nn.sigmoid(gate_act)
    silu_val = gate_act * sigma
    grad_gate = hidden_grad * up_act * sigma * (1.0 + gate_act * (1.0 - sigma))
    grad_up = hidden_grad * silu_val
    return jnp.stack([grad_gate.astype(BF16), grad_up.astype(BF16)])


def body(inputs, target, gate_weight, up_weight, down_weight):
    tok_own = inputs.shape[0]
    offset = (lax.axis_index("z") * NY + lax.axis_index("y")) * tok_own
    target_own = lax.optimization_barrier(lax.dynamic_slice_in_dim(target, offset, tok_own, 0))
    tokens = gather_z(inputs)
    tokens = gather_y(tokens)
    tokens = join(tokens)
    acts, hidden, result = row_phase(
        tokens,
        tok_own,
        lambda val: (matmul(val, gate_weight), matmul(val, up_weight)),
        lambda k, act: (jax.nn.silu(act[0]) * act[1]).astype(BF16)[None],
        lambda full: matmul(full[0], down_weight),
    )
    result_own = scatter_y(split(result))
    result_own = scatter_z(result_own)
    error_own = (result_own - target_own.astype(F32)).astype(BF16)
    output = result_own.astype(BF16)
    errors = gather_z(error_own)
    errors = gather_y(errors)
    errors = join(errors)
    _, grads, input_grad = row_phase(
        errors,
        tok_own,
        lambda val: (contract_last(val, down_weight),),
        lambda k, grad: gate_grads(grad[0], acts[k][0], acts[k][1]),
        lambda full: contract_last(full[0], gate_weight) + contract_last(full[1], up_weight),
    )
    grad_inputs = scatter_y(split(input_grad))
    grad_inputs = scatter_z(grad_inputs).astype(BF16)

    def summed(left, right):
        return sum(contract_first(a, b) for a, b in zip(left, right)).astype(BF16)

    return (
        output,
        grad_inputs,
        summed(tokens, [val[0] for val in grads]),
        summed(tokens, [val[1] for val in grads]),
        summed([val[0] for val in hidden], errors),
    )


def solution(mesh):
    fine = Mesh(mesh.devices.reshape(NX, NC, NZ, NY), AXES)
    row, col = ("x", "core"), ("z", "y")
    placed = (P(col, row), P(None, row), P(row, col), P(row, col), P(col, row))
    return jax.shard_map(
        body,
        mesh=fine,
        in_specs=placed,
        out_specs=(P(col, row), P(col, row), P(row, col), P(row, col), P(col, row)),
        check_vma=False,
    )
```

```python
import jax
import jax.numpy as jnp
from jax import lax
from jax.sharding import Mesh, PartitionSpec as P

F32 = jnp.float32
BF16 = jnp.bfloat16
NX, NC, NZ, NY = 4, 2, 8, 4
AXES = ("x", "core", "z", "y")
CHUNKS = ((0, 1, 2, 3),)


def place(x, core, z, y):
    return ((x * NC + core) * NZ + z) * NY + y


Z_GROUPS = [
    [place(x, core, at ^ (core * NX + x), y) for at in range(NZ)]
    for x in range(NX)
    for core in range(NC)
    for y in range(NY)
]


def contract_first(left, right):
    return lax.dot_general(left, right, (((0,), (0,)), ((), ())), preferred_element_type=F32)


def contract_last(left, right):
    return lax.dot_general(left, right, (((1,), (1,)), ((), ())), preferred_element_type=F32)


def matmul(left, right):
    return jnp.dot(left, right, preferred_element_type=F32)


def shift_y(val, by):
    return lax.ppermute(val, "y", [(at, (at + by) % NY) for at in range(NY)])


def swap_x(val, flip):
    return lax.ppermute(val, "x", [(at, at ^ flip) for at in range(NX)])


def swap_core(val):
    return lax.ppermute(val, "core", [(0, 1), (1, 0)])


def exchange_z(val):
    return lax.all_to_all(
        val, AXES, split_axis=0, concat_axis=0, axis_index_groups=Z_GROUPS, tiled=True
    )


def gather_z(own):
    rows, cols = own.shape
    return exchange_z(jnp.broadcast_to(own[None], (NZ, rows, cols)).reshape(NZ * rows, cols))


def scatter_z(part):
    rows, cols = part.shape
    got = exchange_z(part.astype(BF16)).reshape(NZ, rows // NZ, cols)
    return jnp.sum(got.astype(F32), axis=0)


def gather_y(own):
    half = own.shape[0] // 2
    low = shift_y(own, 1)
    high = shift_y(own, -1)
    far_a = shift_y(low[:half], 1)
    far_b = shift_y(high[half:], -1)
    return [own, low, high, jnp.concatenate([far_a, far_b], axis=0)]


def scatter_y(blocks):
    own, low, high, far = blocks
    half = own.shape[0] // 2
    upper = shift_y(far[:half].astype(BF16), 1)
    lower = shift_y(far[half:].astype(BF16), -1)
    high_b = shift_y(high[half:].astype(BF16), 1)
    low_a = shift_y(low[:half].astype(BF16), -1)
    high_a = shift_y((high[:half] + upper.astype(F32)).astype(BF16), 1)
    low_b = shift_y((low[half:] + lower.astype(F32)).astype(BF16), -1)
    low = jnp.concatenate([low_a, low_b], axis=0)
    high = jnp.concatenate([high_a, high_b], axis=0)
    return own + low.astype(F32) + high.astype(F32)


def after(val, dep):
    return lax.optimization_barrier((val, dep))[0]


def cut(val, tok):
    return val.reshape(-1, NZ, tok, val.shape[1])


def core_step(parts):
    send = jnp.stack([part[:, NX:].astype(BF16) for part in parts])
    return jnp.stack([part[:, :NX] for part in parts]) + swap_core(send).astype(F32)


def x_send(both):
    one, two, three = (both[:, :, flip] for flip in range(1, NX))
    if both.shape[0] == 1:
        return [swap_x(val.astype(BF16), flip) for flip, val in ((1, one), (2, two), (3, three))]
    half = both.shape[1] // 2
    upper = swap_x(two[:, :half].astype(BF16), 1)
    lower = swap_x(two[:, half:].astype(BF16), 3)
    one_a = swap_x(one[:, :half].astype(BF16), 1)
    three_b = swap_x(three[:, half:].astype(BF16), 3)
    three_a = swap_x((three[:, :half] + upper.astype(F32)).astype(BF16), 3)
    one_b = swap_x((one[:, half:] + lower.astype(F32)).astype(BF16), 1)
    return [jnp.concatenate([one_a, one_b], axis=1), jnp.concatenate([three_a, three_b], axis=1)]


def x_sum(both, got):
    total = both[:, :, 0]
    for val in got:
        total = total + val.astype(F32)
    return total


def x_spread(own):
    if own.shape[0] == 1:
        return jnp.stack([own] + [swap_x(own, flip) for flip in range(1, NX)], axis=2)
    half = own.shape[1] // 2
    upper, lower = own[:, :half], own[:, half:]
    one_a = swap_x(upper, 1)
    three_b = swap_x(lower, 3)
    one_b = swap_x(lower, 1)
    three_a = swap_x(upper, 3)
    two_a = swap_x(one_a, 3)
    two_b = swap_x(three_b, 1)
    pairs = ((upper, lower), (one_a, one_b), (two_a, two_b), (three_a, three_b))
    return jnp.stack([jnp.concatenate(val, axis=1) for val in pairs], axis=2)


def core_spread(mine):
    full = jnp.concatenate([mine, swap_core(mine)], axis=2)
    return [val.reshape(-1, val.shape[-1]) for val in full]


def row_phase(chunks, tok, first, middle, last):
    order = range(len(chunks))
    both, own, full, out = [], [], [], []
    for k in order:
        tokens = chunks[k] if k == 0 else after(chunks[k], both[k - 1])
        both.append(core_step([cut(part, tok) for part in first(tokens)]))
    sums = []
    for k in order:
        sums.append(x_sum(both[k], x_send(both[k])))
        own.append(middle(k, sums[k]))
    for k in order:
        full.append(core_spread(x_spread(own[k])))
    for k in order:
        out.append(last(full[k]))
    return sums, full, out


def join(blocks):
    return [
        jnp.concatenate([blocks[at] for at in chunk], axis=0) if len(chunk) > 1 else blocks[chunk[0]]
        for chunk in CHUNKS
    ]


def split(parts):
    blocks = {}
    for chunk, part in zip(CHUNKS, parts):
        rows = part.shape[0] // len(chunk)
        for at, which in enumerate(chunk):
            blocks[which] = part[at * rows : (at + 1) * rows]
    return [blocks[at] for at in range(NY)]


def gate_grads(hidden_grad, gate_act, up_act):
    sigma = jax.nn.sigmoid(gate_act)
    silu_val = gate_act * sigma
    grad_gate = hidden_grad * up_act * sigma * (1.0 + gate_act * (1.0 - sigma))
    grad_up = hidden_grad * silu_val
    return jnp.stack([grad_gate.astype(BF16), grad_up.astype(BF16)])


def body(inputs, target, gate_weight, up_weight, down_weight):
    tok_own = inputs.shape[0]
    offset = (lax.axis_index("z") * NY + lax.axis_index("y")) * tok_own
    target_own = lax.optimization_barrier(lax.dynamic_slice_in_dim(target, offset, tok_own, 0))
    tokens = gather_z(inputs)
    tokens = gather_y(tokens)
    tokens = join(tokens)
    acts, hidden, result = row_phase(
        tokens,
        tok_own,
        lambda val: (matmul(val, gate_weight), matmul(val, up_weight)),
        lambda k, act: (jax.nn.silu(act[0]) * act[1]).astype(BF16)[None],
        lambda full: matmul(full[0], down_weight),
    )
    result_own = scatter_y(split(result))
    result_own = scatter_z(result_own)
    error_own = (result_own - target_own.astype(F32)).astype(BF16)
    output = result_own.astype(BF16)
    errors = gather_z(error_own)
    errors = gather_y(errors)
    errors = join(errors)
    _, grads, input_grad = row_phase(
        errors,
        tok_own,
        lambda val: (contract_last(val, down_weight),),
        lambda k, grad: gate_grads(grad[0], acts[k][0], acts[k][1]),
        lambda full: contract_last(full[0], gate_weight) + contract_last(full[1], up_weight),
    )
    grad_inputs = scatter_y(split(input_grad))
    grad_inputs = scatter_z(grad_inputs).astype(BF16)

    def summed(left, right):
        return sum(contract_first(a, b) for a, b in zip(left, right)).astype(BF16)

    return (
        output,
        grad_inputs,
        summed(tokens, [val[0] for val in grads]),
        summed(tokens, [val[1] for val in grads]),
        summed([val[0] for val in hidden], errors),
    )


def solution(mesh):
    fine = Mesh(mesh.devices.reshape(NX, NC, NZ, NY), AXES)
    row, col = ("x", "core"), ("z", "y")
    placed = (P(col, row), P(None, row), P(row, col), P(row, col), P(col, row))
    return jax.shard_map(
        body,
        mesh=fine,
        in_specs=placed,
        out_specs=(P(col, row), P(col, row), P(row, col), P(row, col), P(col, row)),
        check_vma=False,
    )
```
